32 devices in a mesh: ep: 8 (over z, x), rep: 4 (over y, core).
Axes of the slice: x: 2, y: 2, z: 4, core: 2. Of those that a mesh axis runs over, the one named last changes fastest.
Arguments:
- quant_in: bfloat16 [8, 7168, 2048], P('ep', 'rep'), may hold values from -1 to 1
- scale_in: float32 [8, 56, 16], P('ep', 'rep'), may hold values from 0.002 to 0.02
- b_train: bfloat16 [8, 7168, 64], P('ep', None, 'rep'), may hold values from -0.041992188 to 0.041992188
- a_train: bfloat16 [8, 64, 2048], P('ep', 'rep'), may hold values from -0.59765625 to 0.59765625
- adapter_ranks: int32 [8], replicated, may hold values from 0 to 64
- trainer_map: int32 [8], replicated, may hold values from 0 to 7, each once
- hot_plan: int32 [4], replicated, may hold values from 0 to 7, as said below
Outputs:
- quant_out: bfloat16 [8, 7168, 2048], P('ep', 'rep')
- scale_out: float32 [8, 56, 16], P('ep', 'rep')
- hot_values: bfloat16 [4, 7168, 2048], P(None, ('rep', 'ep'))
- replica_block_scales: float32 [4, 56, 16], P(None, 'rep')
The draws below stay inside these ranges and needn't reach their ends.
Inputs may be any that keep to these rules, and one draw needn't show every extreme that they name: `hot_plan`: 4 distinct expert numbers.
All inputs are finite; a program needn't handle non-finite values. Where the reference program divides by a largest or mean magnitude, that divisor is 1e-20 or more.
Results may differ from the reference program's by a relative error of at most 0.001.
Values may be sent and summed in bfloat16 or wider, within the bound.
A program may use at most 128 MiB of HBM per device.

```python
import math
import jax
import jax.numpy as jnp
from jax import lax

D = 7168
FF = 2048
BLOCK = 128
RMAX = 64
E = 8
HOT = 4


def draw_hot_plan(key, part):
    middle = jax.random.permutation(jax.random.fold_in(key, 17), E - 2).astype(jnp.int32) + 1
    ends = jnp.array([0, E - 1], dtype=jnp.int32)
    chosen = jnp.concatenate([ends, middle[:HOT - 2]])
    shuffle = jax.random.permutation(jax.random.fold_in(key, 29), HOT)
    return chosen[shuffle].astype(jnp.int32)


def place_ends(drawn, stream_key, smallest, top_value):
    spot = [jax.random.randint(jax.random.fold_in(stream_key, axis), (), 0, length) for axis, length in enumerate(drawn.shape)]
    longest = drawn.shape.index(max(drawn.shape))
    beside = spot[:longest] + [(spot[longest] + 1) % drawn.shape[longest]] + spot[longest + 1:]
    return drawn.at[tuple(spot)].set(smallest).at[tuple(beside)].set(top_value)


def shard_levels(key, extent, shards, low, largest):
    loudness = 1.0
    for dim, parts in shards:
        steps = jax.random.uniform(jax.random.fold_in(jax.random.fold_in(key, 6), dim), (parts,), jnp.float32, low / len(shards), largest / len(shards))
        loudness = loudness * jnp.repeat(jnp.exp(steps), extent[dim] // parts).reshape((-1,) + (1,) * (len(extent) - 1 - dim))
    return loudness


def gaussian(key, dims, width, most, cuts=(), kind=jnp.bfloat16):
    values = jax.random.normal(key, dims, jnp.float32) * width
    if len(cuts) > 0:
        values = shard_levels(key, dims, cuts, -0.22, 0.18) * values
    return jnp.clip(values, min=-most, max=most).astype(kind)


def setup_inputs(seed: int = 0) -> dict:
    seeds = jax.random.split(jax.random.key(seed), 8)
    return {
        "quant_in": jnp.clip(jax.random.uniform(seeds[0], (E, D, FF), jnp.float32, -1.0, 1.0) * shard_levels(seeds[0], (E, D, FF), ((0, 8), (1, 4)), -0.4, 0.0), -1.0, 1.0).astype(jnp.bfloat16),
        "scale_in": jnp.clip(jnp.exp(math.log(0.02) - 2.30258502 * jax.random.uniform(seeds[1], (E, D // BLOCK, FF // BLOCK), jnp.float32) ** shard_levels(seeds[1], (E, D // BLOCK, FF // BLOCK), ((0, 8), (1, 4)), -0.2, 0.2)), 0.002, 0.02),
        "b_train": gaussian(seeds[2], (E, D, RMAX), 0.007, 0.041992188, ((0, 8), (2, 4))),
        "a_train": gaussian(seeds[3], (E, RMAX, FF), 0.1, 0.59765625, ((0, 8), (1, 4))),
        "adapter_ranks": place_ends(jax.random.randint(seeds[4], (E,), 0, RMAX + 1), jax.random.fold_in(seeds[4], 1), 0, RMAX).astype(jnp.int32),
        "trainer_map": jax.random.permutation(seeds[5], E).astype(jnp.int32),
        "hot_plan": draw_hot_plan(jax.random.fold_in(seeds[7], 71), 0),
    }


EPS = 1e-6


def reference(quant_in, scale_in, b_train, a_train, adapter_ranks, trainer_map, hot_plan):
    row_blocks = D // BLOCK
    col_blocks = FF // BLOCK
    serving_up_factor = jnp.zeros_like(b_train).at[trainer_map].set(b_train)
    a_serv = jnp.zeros_like(a_train).at[trainer_map].set(a_train)

    def merge_one(items):
        values, scales, b_one, a_one, rank_one = items
        live = (jnp.arange(RMAX, dtype=jnp.int32) < rank_one).astype(jnp.bfloat16)
        active_down_factor = a_one * live[:, None]
        weight_update = jnp.dot(b_one, active_down_factor, preferred_element_type=jnp.float32)
        expert_weight_tensor = values.astype(jnp.float32).reshape(row_blocks, BLOCK, col_blocks, BLOCK) * scales[:, None, :, None]
        merged = expert_weight_tensor + weight_update.reshape(row_blocks, BLOCK, col_blocks, BLOCK)
        scale_new = jnp.max(jnp.abs(merged), axis=(1, 3)) + EPS
        quant_new = (merged / scale_new[:, None, :, None]).reshape(D, FF).astype(jnp.bfloat16)
        return quant_new, scale_new

    quant_out, scale_out = lax.map(merge_one, (quant_in, scale_in, serving_up_factor, a_serv, adapter_ranks))
    hot_values = quant_out[hot_plan]
    replica_block_scales = scale_out[hot_plan]
    return quant_out, scale_out, hot_values, replica_block_scales
```

```python
import functools
import itertools
import math

import jax
import jax.numpy as jnp
from jax import lax
from jax.experimental import pallas as pl
from jax.experimental.pallas import tpu as pltpu
from jax.sharding import PartitionSpec as P

BLOCK = 128
RMAX = 64


EPS = 1e-06
MAX_PLANS = 0
MESH = pl.DeviceIdType.MESH


def exchange_kernel(n, reps, pieces, wide, cols, inv, b_ref, a_ref, bt_out, a_out,
                    b_mid, a_mid, b_stage, a_stage,
                    sb1, rb1, sa1, ra1, sb2, rb2, sa2, ra2):
    ep = lax.axis_index("ep")
    rep = lax.axis_index("rep")
    slab = pieces * wide
    barrier = pltpu.get_barrier_semaphore()
    for de in range(n):
        for dr in range(reps):
            if de or dr:
                pl.semaphore_signal(
                    barrier,
                    inc=1,
                    device_id={"ep": lax.rem(ep + de, n), "rep": lax.rem(rep + dr, reps)},
                    device_id_type=MESH,
                )
    pl.semaphore_wait(barrier, n * reps - 1)

    def move(own, src, dst, send, recv, de, dr):
        if own:
            return pltpu.make_async_copy(src, dst, recv)
        return pltpu.make_async_remote_copy(
            src_ref=src,
            dst_ref=dst,
            send_sem=send,
            recv_sem=recv,
            device_id={"ep": lax.rem(ep + de, n), "rep": lax.rem(rep + dr, reps)},
            device_id_type=MESH,
        )

    def b_first(de, dr):
        j, q = lax.rem(ep + de, n), lax.rem(rep + dr, reps)
        at = q * slab + jnp.minimum(j, pieces - 1) * wide
        src = b_ref.at[0, :, pl.ds(pl.multiple_of(at, BLOCK), wide)]
        return j, move(not (de or dr), src, b_mid.at[ep, rep], sb1.at[de, dr], rb1.at[ep, rep], de, dr)

    def a_first(de):
        j = lax.rem(ep + de, n)
        src = a_ref.at[0, :, pl.ds(pl.multiple_of(j * cols, cols), cols)]
        return move(de == 0, src, a_mid.at[ep], sa1.at[de], ra1.at[ep], de, 0)

    order = [(de, dr) for de in reversed(range(n)) for dr in range(reps)]
    for de in reversed(range(n)):
        a_first(de).start()
    for de, dr in order:
        j, copy = b_first(de, dr)
        pl.when(j < pieces)(copy.start)

    for s in range(n):
        pltpu.make_async_copy(a_mid.at[s], a_mid.at[s], ra1.at[s]).wait()
    for d in range(n):
        a_stage[d] = a_mid[inv[d]]

    def a_second(de, dr):
        d = lax.rem(ep + de, n)
        dst = a_out.at[rep, :, pl.ds(pl.multiple_of(ep * cols, cols), cols)]
        return move(not (de or dr), a_stage.at[d], dst, sa2.at[de, dr], ra2.at[ep, rep], de, dr)

    def b_second(de):
        d = lax.rem(ep + de, n)
        here = jnp.minimum(ep, pieces - 1)
        dst = bt_out.at[:, :, pl.ds(pl.multiple_of(here * wide, wide), wide)]
        return move(de == 0, b_stage.at[d], dst, sb2.at[de], rb2.at[ep], de, 0)

    for de, dr in order:
        a_second(de, dr).start()

    @pl.when(ep < pieces)
    def _():
        for s in range(n):
            for r in range(reps):
                pltpu.make_async_copy(b_mid.at[s, r], b_mid.at[s, r], rb1.at[s, r]).wait()
        for d in range(n):
            b_stage[d] = b_mid[inv[d]]
        for de in reversed(range(n)):
            b_second(de).start()

    for j in range(n):
        for q in range(reps):
            dst = a_out.at[q, :, pl.ds(j * cols, cols)]
            pltpu.make_async_copy(dst, dst, ra2.at[j, q]).wait()
    for j in range(pieces):
        dst = bt_out.at[:, :, pl.ds(j * wide, wide)]
        pltpu.make_async_copy(dst, dst, rb2.at[j]).wait()
    for de, dr in order:
        if de or dr:
            j, copy = b_first(de, dr)
            pl.when(j < pieces)(copy.wait_send)
            a_second(de, dr).wait_send()
    for de in range(1, n):
        a_first(de).wait_send()
        copy = b_second(de)
        pl.when(ep < pieces)(copy.wait_send)


def exchange(inv, b_train, a_train, n, reps):
    depth, ranks = b_train.shape[1:]
    features = a_train.shape[2]
    slab = depth // reps
    blocks = slab // BLOCK
    wide = -(-blocks // n) * BLOCK
    pieces = slab // wide
    cols = features // n
    bf16 = jnp.bfloat16
    dma = pltpu.SemaphoreType.DMA
    return pl.pallas_call(
        functools.partial(exchange_kernel, n, reps, pieces, wide, cols),
        out_shape=(
            jax.ShapeDtypeStruct((reps, ranks, slab), bf16),
            jax.ShapeDtypeStruct((reps, ranks, features), bf16),
        ),
        in_specs=[
            pl.BlockSpec(memory_space=pltpu.SMEM),
            pl.BlockSpec(memory_space=pltpu.VMEM),
            pl.BlockSpec(memory_space=pltpu.VMEM),
        ],
        out_specs=(pl.BlockSpec(memory_space=pltpu.VMEM),) * 2,
        scratch_shapes=[
            pltpu.VMEM((n, reps, ranks, wide), bf16),
            pltpu.VMEM((n, ranks, cols), bf16),
            pltpu.VMEM((n, reps, ranks, wide), bf16),
            pltpu.VMEM((n, ranks, cols), bf16),
            dma((n, reps)), dma((n, reps)), dma((n,)), dma((n,)),
            dma((n,)), dma((n,)), dma((n, reps)), dma((n, reps)),
        ],
        compiler_params=pltpu.CompilerParams(
            collective_id=0, has_side_effects=True, vmem_limit_bytes=32 << 20
        ),
        name="exchange",
    )(inv, jnp.swapaxes(b_train, 1, 2), a_train)


def merge_kernel(rank, scale_in, quant_in, bt, a, quant_out, scale_out, live):
    step = pl.program_id(0)
    blocks = quant_in.shape[1] // BLOCK
    col_blocks = quant_in.shape[2] // BLOCK

    @pl.when(step == 0)
    def _():
        keep = lax.broadcasted_iota(jnp.int32, live.shape, 0) < rank[0]
        live[...] = jnp.where(keep, a[...].astype(jnp.float32), 0.0).astype(jnp.bfloat16)

    lane = lax.broadcasted_iota(jnp.int32, (1, col_blocks), 1)
    for i in range(blocks):
        delta = lax.dot_general(
            bt[:, i * BLOCK:(i + 1) * BLOCK], live[...], (((0,), (0,)), ((), ())),
            preferred_element_type=jnp.float32,
        )
        rows = slice(i * BLOCK, (i + 1) * BLOCK)
        found = jnp.zeros((1, col_blocks), jnp.float32)
        for c in range(col_blocks):
            cut = slice(c * BLOCK, (c + 1) * BLOCK)
            held = quant_in[0, rows, cut].astype(jnp.float32)
            merged = held * scale_in[0, step * blocks + i, c] + delta[:, cut]
            top = jnp.max(jnp.max(jnp.abs(merged), axis=0, keepdims=True), axis=1, keepdims=True) + EPS
            quant_out[0, rows, cut] = (merged * (1.0 / top)).astype(jnp.bfloat16)
            found = jnp.where(lane == c, top, found)
        scale_out[0, pl.ds(step * blocks + i, 1), :] = found


def merge(rank, scale_in, quant_in, bt, a):
    _, rows, features = quant_in.shape
    total = rows // BLOCK
    blocks = 2 if total % 2 == 0 else 1
    steps = total // blocks
    tall = blocks * BLOCK
    return pl.pallas_call(
        merge_kernel,
        grid=(steps,),
        out_shape=(
            jax.ShapeDtypeStruct(quant_in.shape, jnp.bfloat16),
            jax.ShapeDtypeStruct(scale_in.shape, jnp.float32),
        ),
        in_specs=[
            pl.BlockSpec(memory_space=pltpu.SMEM),
            pl.BlockSpec(memory_space=pltpu.SMEM),
            pl.BlockSpec((1, tall, features), lambda i: (0, i, 0)),
            pl.BlockSpec((bt.shape[0], tall), lambda i: (0, i)),
            pl.BlockSpec(a.shape, lambda i: (0, 0)),
        ],
        out_specs=(
            pl.BlockSpec((1, tall, features), lambda i: (0, i, 0)),
            pl.BlockSpec(scale_in.shape, lambda i: (0, 0, 0)),
        ),
        scratch_shapes=[pltpu.VMEM(a.shape, jnp.bfloat16)],
        compiler_params=pltpu.CompilerParams(vmem_limit_bytes=32 << 20),
        name="merge",
    )(rank, scale_in, quant_in, bt, a)


def hot_kernel(n, sources, piece, quant, scale, slots, scales, send, recv, ssend, srecv):
    ep = lax.axis_index("ep")
    barrier = pltpu.get_barrier_semaphore()
    for de in range(1, n):
        pl.semaphore_signal(
            barrier, inc=1, device_id={"ep": lax.rem(ep + de, n)}, device_id_type=MESH
        )
    pl.semaphore_wait(barrier, n - 1)

    def scale_copy(de):
        return pltpu.make_async_remote_copy(
            src_ref=scale, dst_ref=scales.at[pl.ds(ep, 1)], send_sem=ssend.at[de],
            recv_sem=srecv.at[ep], device_id={"ep": lax.rem(ep + de, n)}, device_id_type=MESH,
        )

    def piece_copy(k, p):
        return pltpu.make_async_remote_copy(
            src_ref=quant.at[0, pl.ds(p * piece, piece)], dst_ref=slots.at[k],
            send_sem=send.at[p], recv_sem=recv.at[k], device_id={"ep": p}, device_id_type=MESH,
        )

    def own_copy(k, p):
        return pltpu.make_async_copy(quant.at[0, pl.ds(p * piece, piece)], slots.at[k], recv.at[k])

    own_scale = pltpu.make_async_copy(scale, scales.at[pl.ds(ep, 1)], srecv.at[ep])
    own_scale.start()
    for de in range(1, n):
        scale_copy(de).start()
    for k, e in enumerate(sources):
        @pl.when(ep == e)
        def _():
            for p in range(n):
                if p != e:
                    piece_copy(k, p).start()
            own_copy(k, e).start()
    for k in range(len(sources)):
        pltpu.make_async_copy(slots.at[k], slots.at[k], recv.at[k]).wait()
    for k, e in enumerate(sources):
        @pl.when(ep == e)
        def _():
            for p in range(n):
                if p != e:
                    piece_copy(k, p).wait_send()
    for s in range(n):
        pltpu.make_async_copy(scales.at[pl.ds(s, 1)], scales.at[pl.ds(s, 1)], srecv.at[s]).wait()
    for de in range(1, n):
        scale_copy(de).wait_send()


def spread(quant, scale, n, sources, collective_id):
    piece = quant.shape[1] // n
    dma = pltpu.SemaphoreType.DMA
    return pl.pallas_call(
        functools.partial(hot_kernel, n, sources, piece),
        out_shape=(
            jax.ShapeDtypeStruct((len(sources), piece, quant.shape[2]), quant.dtype),
            jax.ShapeDtypeStruct((n,) + scale.shape[1:], scale.dtype),
        ),
        in_specs=[
            pl.BlockSpec(memory_space=pl.ANY),
            pl.BlockSpec(memory_space=pltpu.VMEM),
        ],
        out_specs=(
            pl.BlockSpec(memory_space=pl.ANY),
            pl.BlockSpec(memory_space=pltpu.VMEM),
        ),
        scratch_shapes=[dma((n,)), dma((len(sources),)), dma((n,)), dma((n,))],
        compiler_params=pltpu.CompilerParams(collective_id=collective_id, has_side_effects=True),
        name="spread",
    )(quant, scale)


def place_kernel(where, plan, held, scales, values, picked):
    values[...] = held[...]

    @pl.when(pl.program_id(0) == 0)
    def _():
        for k in range(picked.shape[0]):
            picked[k] = scales[plan[k]]


def place(where, plan, slots, scales):
    count = plan.shape[0]
    block = (1,) + slots.shape[1:]
    return pl.pallas_call(
        place_kernel,
        grid_spec=pltpu.PrefetchScalarGridSpec(
            num_scalar_prefetch=2,
            grid=(count,),
            in_specs=[
                pl.BlockSpec(block, lambda k, where, plan: (where[k], 0, 0)),
                pl.BlockSpec(scales.shape, lambda k, where, plan: (0, 0, 0)),
            ],
            out_specs=[
                pl.BlockSpec(block, lambda k, where, plan: (k, 0, 0)),
                pl.BlockSpec((count,) + scales.shape[1:], lambda k, where, plan: (0, 0, 0)),
            ],
        ),
        out_shape=(
            jax.ShapeDtypeStruct((count,) + slots.shape[1:], slots.dtype),
            jax.ShapeDtypeStruct((count,) + scales.shape[1:], scales.dtype),
        ),
        compiler_params=pltpu.CompilerParams(vmem_limit_bytes=32 << 20),
        name="place",
    )(where, plan, slots, scales)


def kernel_body(n, reps, quant_in, scale_in, b_train, a_train, adapter_ranks, trainer_map, hot_plan):
    owner = lax.axis_index("ep")
    serving = jnp.arange(n, dtype=jnp.int32)
    inv = jnp.sum(
        jnp.where(trainer_map[None, :] == serving[:, None], serving[None, :], 0), axis=1
    ).astype(jnp.int32)
    bt, a = exchange(inv, b_train, a_train, n, reps)
    bt = bt.reshape(-1, bt.shape[2])
    a = a.reshape(-1, a.shape[2])
    rank = lax.dynamic_slice_in_dim(adapter_ranks, owner, 1, 0)
    quant_out, scale_out = merge(rank, scale_in, quant_in, bt, a)
    count = hot_plan.shape[0]
    plans = list(itertools.combinations(range(n), count))
    if len(plans) <= MAX_PLANS:
        table = [0] * (1 << n)
        for at, chosen in enumerate(plans):
            table[sum(1 << e for e in chosen)] = at
        which = jnp.asarray(table, jnp.int32)[jnp.sum(jnp.left_shift(1, hot_plan))]
        branches = [
            functools.partial(spread, n=n, sources=chosen, collective_id=1 + at)
            for at, chosen in enumerate(plans)
        ]
        slots, scales = lax.switch(which, branches, quant_out, scale_out)
        where = jnp.sum((hot_plan[None, :] < hot_plan[:, None]).astype(jnp.int32), axis=1)
    else:
        slots, scales = spread(quant_out, scale_out, n, tuple(range(n)), 1)
        where = hot_plan
    hot_values, replica_block_scales = place(where.astype(jnp.int32), hot_plan, slots, scales)
    return quant_out, scale_out, hot_values, replica_block_scales


def fits(n, reps, quant_in, scale_in, b_train, a_train):
    slab = b_train[1] // reps
    blocks = slab // BLOCK
    wide = -(-blocks // n)
    return (
        quant_in[0] == n
        and blocks * BLOCK == slab
        and blocks % wide == 0
        and (b_train[2] // reps) % 16 == 0
        and a_train[2] % (n * BLOCK) == 0
        and (slab // n) % 16 == 0
    )


def body(quant_in, scale_in, b_train, a_train, adapter_ranks, trainer_map, hot_plan):
    exp_dev = quant_in.shape[0]
    rows = quant_in.shape[1]
    cols = quant_in.shape[2]
    owner = lax.axis_index("ep")
    owned_expert_index = owner * exp_dev + jnp.arange(exp_dev, dtype=jnp.int32)
    b_rows = lax.all_to_all(b_train, "rep", split_axis=1, concat_axis=2, tiled=True)
    a_full = lax.all_gather(a_train, "rep", axis=1, tiled=True)
    rank_selector = (trainer_map[None, :] == owned_expert_index[:, None]).astype(jnp.bfloat16)
    b_sum = jnp.einsum(
        "ji,idr->jdr",
        rank_selector,
        lax.all_gather(b_rows, "ep", axis=0, tiled=True),
        preferred_element_type=jnp.float32,
    )
    a_sum = jnp.einsum(
        "ji,irf->jrf",
        rank_selector,
        lax.all_gather(a_full, "ep", axis=0, tiled=True),
        preferred_element_type=jnp.float32,
    )
    serving_up_factor = b_sum.astype(jnp.bfloat16)
    a_serv = a_sum.astype(jnp.bfloat16)
    local_rank_indices = lax.dynamic_slice_in_dim(adapter_ranks, owner * exp_dev, exp_dev, 0)
    live = (jnp.arange(RMAX, dtype=jnp.int32)[None, :] < local_rank_indices[:, None]).astype(
        jnp.bfloat16
    )
    active_down_factor = a_serv * live[:, :, None]
    weight_update = jnp.einsum(
        "enw,ewk->enk", serving_up_factor, active_down_factor, preferred_element_type=jnp.float32
    )
    row_blocks = rows // BLOCK
    col_blocks = cols // BLOCK
    expert_weight_tensor = (
        quant_in.astype(jnp.float32).reshape(exp_dev, row_blocks, BLOCK, col_blocks, BLOCK)
        * scale_in[:, :, None, :, None]
    )
    merged = expert_weight_tensor + weight_update.reshape(
        exp_dev, row_blocks, BLOCK, col_blocks, BLOCK
    )
    scale_out = jnp.max(jnp.abs(merged), axis=(2, 4)) + EPS
    quant_out = (
        (merged / scale_out[:, :, None, :, None]).reshape(exp_dev, rows, cols).astype(jnp.bfloat16)
    )
    received = lax.all_to_all(quant_out, "ep", split_axis=1, concat_axis=0, tiled=True)
    total = received.shape[0]
    rank_selector = (hot_plan[:, None] == jnp.arange(total, dtype=jnp.int32)[None, :]).astype(
        jnp.bfloat16
    )
    hot_values = jnp.einsum(
        "je,edf->jdf", rank_selector, received, preferred_element_type=jnp.float32
    ).astype(jnp.bfloat16)
    all_scales = lax.all_gather(scale_out, "ep", axis=0, tiled=True)
    every = all_scales.shape[0]
    scale_select = (hot_plan[:, None] == jnp.arange(every, dtype=jnp.int32)[None, :]).astype(
        jnp.float32
    )
    replica_block_scales = jnp.einsum(
        "je,ebc->jbc", scale_select, all_scales, precision=lax.Precision.HIGHEST
    )
    return (quant_out, scale_out, hot_values, replica_block_scales)


def solution(mesh):
    n, reps = mesh.shape["ep"], mesh.shape["rep"]

    placed = (
        P("ep", "rep", None),
        P("ep", "rep", None),
        P("ep", None, "rep"),
        P("ep", "rep", None),
        P(),
        P(),
        P(),
    )
    outs = (
        P("ep", "rep", None),
        P("ep", "rep", None),
        P(None, ("rep", "ep"), None),
        P(None, "rep", None),
    )

    def run(quant_in, scale_in, b_train, a_train, adapter_ranks, trainer_map, hot_plan):
        shapes = [v.shape for v in (quant_in, scale_in, b_train, a_train)]
        local = functools.partial(kernel_body, n, reps) if fits(n, reps, *shapes) else body
        step = jax.shard_map(local, mesh=mesh, in_specs=placed, out_specs=outs, check_vma=False)
        return step(quant_in, scale_in, b_train, a_train, adapter_ranks, trainer_map, hot_plan)

    return run
```

```python
import functools
import itertools
import math

import jax
import jax.numpy as jnp
from jax import lax
from jax.experimental import pallas as pl
from jax.experimental.pallas import tpu as pltpu
from jax.sharding import PartitionSpec as P

BLOCK = 128
RMAX = 64


EPS = 1e-06
MAX_PLANS = 128
MESH = pl.DeviceIdType.MESH


def exchange_kernel(n, reps, pieces, wide, cols, inv, b_ref, a_ref, bt_out, a_out,
                    b_mid, a_mid, b_stage, a_stage,
                    sb1, rb1, sa1, ra1, sb2, rb2, sa2, ra2):
    ep = lax.axis_index("ep")
    rep = lax.axis_index("rep")
    slab = pieces * wide
    barrier = pltpu.get_barrier_semaphore()
    for de in range(n):
        for dr in range(reps):
            if de or dr:
                pl.semaphore_signal(
                    barrier,
                    inc=1,
                    device_id={"ep": lax.rem(ep + de, n), "rep": lax.rem(rep + dr, reps)},
                    device_id_type=MESH,
                )
    pl.semaphore_wait(barrier, n * reps - 1)

    def move(own, src, dst, send, recv, de, dr):
        if own:
            return pltpu.make_async_copy(src, dst, recv)
        return pltpu.make_async_remote_copy(
            src_ref=src,
            dst_ref=dst,
            send_sem=send,
            recv_sem=recv,
            device_id={"ep": lax.rem(ep + de, n), "rep": lax.rem(rep + dr, reps)},
            device_id_type=MESH,
        )

    def b_first(de, dr):
        j, q = lax.rem(ep + de, n), lax.rem(rep + dr, reps)
        at = q * slab + jnp.minimum(j, pieces - 1) * wide
        src = b_ref.at[0, :, pl.ds(pl.multiple_of(at, BLOCK), wide)]
        return j, move(not (de or dr), src, b_mid.at[ep, rep], sb1.at[de, dr], rb1.at[ep, rep], de, dr)

    def a_first(de):
        j = lax.rem(ep + de, n)
        src = a_ref.at[0, :, pl.ds(pl.multiple_of(j * cols, cols), cols)]
        return move(de == 0, src, a_mid.at[ep], sa1.at[de], ra1.at[ep], de, 0)

    order = [(de, dr) for de in reversed(range(n)) for dr in range(reps)]
    for de in reversed(range(n)):
        a_first(de).start()
    for de, dr in order:
        j, copy = b_first(de, dr)
        pl.when(j < pieces)(copy.start)

    for s in range(n):
        pltpu.make_async_copy(a_mid.at[s], a_mid.at[s], ra1.at[s]).wait()
    for d in range(n):
        a_stage[d] = a_mid[inv[d]]

    def a_second(de, dr):
        d = lax.rem(ep + de, n)
        dst = a_out.at[rep, :, pl.ds(pl.multiple_of(ep * cols, cols), cols)]
        return move(not (de or dr), a_stage.at[d], dst, sa2.at[de, dr], ra2.at[ep, rep], de, dr)

    def b_second(de):
        d = lax.rem(ep + de, n)
        here = jnp.minimum(ep, pieces - 1)
        dst = bt_out.at[:, :, pl.ds(pl.multiple_of(here * wide, wide), wide)]
        return move(de == 0, b_stage.at[d], dst, sb2.at[de], rb2.at[ep], de, 0)

    for de, dr in order:
        a_second(de, dr).start()

    @pl.when(ep < pieces)
    def _():
        for s in range(n):
            for r in range(reps):
                pltpu.make_async_copy(b_mid.at[s, r], b_mid.at[s, r], rb1.at[s, r]).wait()
        for d in range(n):
            b_stage[d] = b_mid[inv[d]]
        for de in reversed(range(n)):
            b_second(de).start()

    for j in range(n):
        for q in range(reps):
            dst = a_out.at[q, :, pl.ds(j * cols, cols)]
            pltpu.make_async_copy(dst, dst, ra2.at[j, q]).wait()
    for j in range(pieces):
        dst = bt_out.at[:, :, pl.ds(j * wide, wide)]
        pltpu.make_async_copy(dst, dst, rb2.at[j]).wait()
    for de, dr in order:
        if de or dr:
            j, copy = b_first(de, dr)
            pl.when(j < pieces)(copy.wait_send)
            a_second(de, dr).wait_send()
    for de in range(1, n):
        a_first(de).wait_send()
        copy = b_second(de)
        pl.when(ep < pieces)(copy.wait_send)


def exchange(inv, b_train, a_train, n, reps):
    depth, ranks = b_train.shape[1:]
    features = a_train.shape[2]
    slab = depth // reps
    blocks = slab // BLOCK
    wide = -(-blocks // n) * BLOCK
    pieces = slab // wide
    cols = features // n
    bf16 = jnp.bfloat16
    dma = pltpu.SemaphoreType.DMA
    return pl.pallas_call(
        functools.partial(exchange_kernel, n, reps, pieces, wide, cols),
        out_shape=(
            jax.ShapeDtypeStruct((reps, ranks, slab), bf16),
            jax.ShapeDtypeStruct((reps, ranks, features), bf16),
        ),
        in_specs=[
            pl.BlockSpec(memory_space=pltpu.SMEM),
            pl.BlockSpec(memory_space=pltpu.VMEM),
            pl.BlockSpec(memory_space=pltpu.VMEM),
        ],
        out_specs=(pl.BlockSpec(memory_space=pltpu.VMEM),) * 2,
        scratch_shapes=[
            pltpu.VMEM((n, reps, ranks, wide), bf16),
            pltpu.VMEM((n, ranks, cols), bf16),
            pltpu.VMEM((n, reps, ranks, wide), bf16),
            pltpu.VMEM((n, ranks, cols), bf16),
            dma((n, reps)), dma((n, reps)), dma((n,)), dma((n,)),
            dma((n,)), dma((n,)), dma((n, reps)), dma((n, reps)),
        ],
        compiler_params=pltpu.CompilerParams(
            collective_id=0, has_side_effects=True, vmem_limit_bytes=32 << 20
        ),
        name="exchange",
    )(inv, jnp.swapaxes(b_train, 1, 2), a_train)


def merge_kernel(rank, scale_in, quant_in, bt, a, quant_out, scale_out, live):
    step = pl.program_id(0)
    blocks = quant_in.shape[1] // BLOCK
    col_blocks = quant_in.shape[2] // BLOCK

    @pl.when(step == 0)
    def _():
        keep = lax.broadcasted_iota(jnp.int32, live.shape, 0) < rank[0]
        live[...] = jnp.where(keep, a[...].astype(jnp.float32), 0.0).astype(jnp.bfloat16)

    lane = lax.broadcasted_iota(jnp.int32, (1, col_blocks), 1)
    for i in range(blocks):
        delta = lax.dot_general(
            bt[:, i * BLOCK:(i + 1) * BLOCK], live[...], (((0,), (0,)), ((), ())),
            preferred_element_type=jnp.float32,
        )
        rows = slice(i * BLOCK, (i + 1) * BLOCK)
        found = jnp.zeros((1, col_blocks), jnp.float32)
        for c in range(col_blocks):
            cut = slice(c * BLOCK, (c + 1) * BLOCK)
            held = quant_in[0, rows, cut].astype(jnp.float32)
            merged = held * scale_in[0, step * blocks + i, c] + delta[:, cut]
            top = jnp.max(jnp.max(jnp.abs(merged), axis=0, keepdims=True), axis=1, keepdims=True) + EPS
            quant_out[0, rows, cut] = (merged * (1.0 / top)).astype(jnp.bfloat16)
            found = jnp.where(lane == c, top, found)
        scale_out[0, pl.ds(step * blocks + i, 1), :] = found


def merge(rank, scale_in, quant_in, bt, a):
    _, rows, features = quant_in.shape
    total = rows // BLOCK
    blocks = 2 if total % 2 == 0 else 1
    steps = total // blocks
    tall = blocks * BLOCK
    return pl.pallas_call(
        merge_kernel,
        grid=(steps,),
        out_shape=(
            jax.ShapeDtypeStruct(quant_in.shape, jnp.bfloat16),
            jax.ShapeDtypeStruct(scale_in.shape, jnp.float32),
        ),
        in_specs=[
            pl.BlockSpec(memory_space=pltpu.SMEM),
            pl.BlockSpec(memory_space=pltpu.SMEM),
            pl.BlockSpec((1, tall, features), lambda i: (0, i, 0)),
            pl.BlockSpec((bt.shape[0], tall), lambda i: (0, i)),
            pl.BlockSpec(a.shape, lambda i: (0, 0)),
        ],
        out_specs=(
            pl.BlockSpec((1, tall, features), lambda i: (0, i, 0)),
            pl.BlockSpec(scale_in.shape, lambda i: (0, 0, 0)),
        ),
        scratch_shapes=[pltpu.VMEM(a.shape, jnp.bfloat16)],
        compiler_params=pltpu.CompilerParams(vmem_limit_bytes=32 << 20),
        name="merge",
    )(rank, scale_in, quant_in, bt, a)


def hot_kernel(n, sources, piece, quant, scale, slots, scales, send, recv, ssend, srecv):
    ep = lax.axis_index("ep")
    barrier = pltpu.get_barrier_semaphore()
    for de in range(1, n):
        pl.semaphore_signal(
            barrier, inc=1, device_id={"ep": lax.rem(ep + de, n)}, device_id_type=MESH
        )
    pl.semaphore_wait(barrier, n - 1)

    def scale_copy(de):
        return pltpu.make_async_remote_copy(
            src_ref=scale, dst_ref=scales.at[pl.ds(ep, 1)], send_sem=ssend.at[de],
            recv_sem=srecv.at[ep], device_id={"ep": lax.rem(ep + de, n)}, device_id_type=MESH,
        )

    def piece_copy(k, p):
        return pltpu.make_async_remote_copy(
            src_ref=quant.at[0, pl.ds(p * piece, piece)], dst_ref=slots.at[k],
            send_sem=send.at[p], recv_sem=recv.at[k], device_id={"ep": p}, device_id_type=MESH,
        )

    def own_copy(k, p):
        return pltpu.make_async_copy(quant.at[0, pl.ds(p * piece, piece)], slots.at[k], recv.at[k])

    own_scale = pltpu.make_async_copy(scale, scales.at[pl.ds(ep, 1)], srecv.at[ep])
    own_scale.start()
    for de in range(1, n):
        scale_copy(de).start()
    for k, e in enumerate(sources):
        @pl.when(ep == e)
        def _():
            for p in range(n):
                if p != e:
                    piece_copy(k, p).start()
            own_copy(k, e).start()
    for k in range(len(sources)):
        pltpu.make_async_copy(slots.at[k], slots.at[k], recv.at[k]).wait()
    for k, e in enumerate(sources):
        @pl.when(ep == e)
        def _():
            for p in range(n):
                if p != e:
                    piece_copy(k, p).wait_send()
    for s in range(n):
        pltpu.make_async_copy(scales.at[pl.ds(s, 1)], scales.at[pl.ds(s, 1)], srecv.at[s]).wait()
    for de in range(1, n):
        scale_copy(de).wait_send()


def spread(quant, scale, n, sources, collective_id):
    piece = quant.shape[1] // n
    dma = pltpu.SemaphoreType.DMA
    return pl.pallas_call(
        functools.partial(hot_kernel, n, sources, piece),
        out_shape=(
            jax.ShapeDtypeStruct((len(sources), piece, quant.shape[2]), quant.dtype),
            jax.ShapeDtypeStruct((n,) + scale.shape[1:], scale.dtype),
        ),
        in_specs=[
            pl.BlockSpec(memory_space=pl.ANY),
            pl.BlockSpec(memory_space=pltpu.VMEM),
        ],
        out_specs=(
            pl.BlockSpec(memory_space=pl.ANY),
            pl.BlockSpec(memory_space=pltpu.VMEM),
        ),
        scratch_shapes=[dma((n,)), dma((len(sources),)), dma((n,)), dma((n,))],
        compiler_params=pltpu.CompilerParams(collective_id=collective_id, has_side_effects=True),
        name="spread",
    )(quant, scale)


def place_kernel(where, plan, held, scales, values, picked):
    values[...] = held[...]

    @pl.when(pl.program_id(0) == 0)
    def _():
        for k in range(picked.shape[0]):
            picked[k] = scales[plan[k]]


def place(where, plan, slots, scales):
    count = plan.shape[0]
    block = (1,) + slots.shape[1:]
    return pl.pallas_call(
        place_kernel,
        grid_spec=pltpu.PrefetchScalarGridSpec(
            num_scalar_prefetch=2,
            grid=(count,),
            in_specs=[
                pl.BlockSpec(block, lambda k, where, plan: (where[k], 0, 0)),
                pl.BlockSpec(scales.shape, lambda k, where, plan: (0, 0, 0)),
            ],
            out_specs=[
                pl.BlockSpec(block, lambda k, where, plan: (k, 0, 0)),
                pl.BlockSpec((count,) + scales.shape[1:], lambda k, where, plan: (0, 0, 0)),
            ],
        ),
        out_shape=(
            jax.ShapeDtypeStruct((count,) + slots.shape[1:], slots.dtype),
            jax.ShapeDtypeStruct((count,) + scales.shape[1:], scales.dtype),
        ),
        compiler_params=pltpu.CompilerParams(vmem_limit_bytes=32 << 20),
        name="place",
    )(where, plan, slots, scales)


def kernel_body(n, reps, quant_in, scale_in, b_train, a_train, adapter_ranks, trainer_map, hot_plan):
    owner = lax.axis_index("ep")
    serving = jnp.arange(n, dtype=jnp.int32)
    inv = jnp.sum(
        jnp.where(trainer_map[None, :] == serving[:, None], serving[None, :], 0), axis=1
    ).astype(jnp.int32)
    bt, a = exchange(inv, b_train, a_train, n, reps)
    bt = bt.reshape(-1, bt.shape[2])
    a = a.reshape(-1, a.shape[2])
    rank = lax.dynamic_slice_in_dim(adapter_ranks, owner, 1, 0)
    quant_out, scale_out = merge(rank, scale_in, quant_in, bt, a)
    count = hot_plan.shape[0]
    plans = list(itertools.combinations(range(n), count))
    if len(plans) <= MAX_PLANS:
        table = [0] * (1 << n)
        for at, chosen in enumerate(plans):
            table[sum(1 << e for e in chosen)] = at
        which = jnp.asarray(table, jnp.int32)[jnp.sum(jnp.left_shift(1, hot_plan))]
        branches = [
            functools.partial(spread, n=n, sources=chosen, collective_id=1 + at)
            for at, chosen in enumerate(plans)
        ]
        slots, scales = lax.switch(which, branches, quant_out, scale_out)
        where = jnp.sum((hot_plan[None, :] < hot_plan[:, None]).astype(jnp.int32), axis=1)
    else:
        slots, scales = spread(quant_out, scale_out, n, tuple(range(n)), 1)
        where = hot_plan
    hot_values, replica_block_scales = place(where.astype(jnp.int32), hot_plan, slots, scales)
    return quant_out, scale_out, hot_values, replica_block_scales


def fits(n, reps, quant_in, scale_in, b_train, a_train):
    slab = b_train[1] // reps
    blocks = slab // BLOCK
    wide = -(-blocks // n)
    return (
        quant_in[0] == n
        and blocks * BLOCK == slab
        and blocks % wide == 0
        and (b_train[2] // reps) % 16 == 0
        and a_train[2] % (n * BLOCK) == 0
        and (slab // n) % 16 == 0
    )


def body(quant_in, scale_in, b_train, a_train, adapter_ranks, trainer_map, hot_plan):
    exp_dev = quant_in.shape[0]
    rows = quant_in.shape[1]
    cols = quant_in.shape[2]
    owner = lax.axis_index("ep")
    owned_expert_index = owner * exp_dev + jnp.arange(exp_dev, dtype=jnp.int32)
    b_rows = lax.all_to_all(b_train, "rep", split_axis=1, concat_axis=2, tiled=True)
    a_full = lax.all_gather(a_train, "rep", axis=1, tiled=True)
    rank_selector = (trainer_map[None, :] == owned_expert_index[:, None]).astype(jnp.bfloat16)
    b_sum = jnp.einsum(
        "ji,idr->jdr",
        rank_selector,
        lax.all_gather(b_rows, "ep", axis=0, tiled=True),
        preferred_element_type=jnp.float32,
    )
    a_sum = jnp.einsum(
        "ji,irf->jrf",
        rank_selector,
        lax.all_gather(a_full, "ep", axis=0, tiled=True),
        preferred_element_type=jnp.float32,
    )
    serving_up_factor = b_sum.astype(jnp.bfloat16)
    a_serv = a_sum.astype(jnp.bfloat16)
    local_rank_indices = lax.dynamic_slice_in_dim(adapter_ranks, owner * exp_dev, exp_dev, 0)
    live = (jnp.arange(RMAX, dtype=jnp.int32)[None, :] < local_rank_indices[:, None]).astype(
        jnp.bfloat16
    )
    active_down_factor = a_serv * live[:, :, None]
    weight_update = jnp.einsum(
        "enw,ewk->enk", serving_up_factor, active_down_factor, preferred_element_type=jnp.float32
    )
    row_blocks = rows // BLOCK
    col_blocks = cols // BLOCK
    expert_weight_tensor = (
        quant_in.astype(jnp.float32).reshape(exp_dev, row_blocks, BLOCK, col_blocks, BLOCK)
        * scale_in[:, :, None, :, None]
    )
    merged = expert_weight_tensor + weight_update.reshape(
        exp_dev, row_blocks, BLOCK, col_blocks, BLOCK
    )
    scale_out = jnp.max(jnp.abs(merged), axis=(2, 4)) + EPS
    quant_out = (
        (merged / scale_out[:, :, None, :, None]).reshape(exp_dev, rows, cols).astype(jnp.bfloat16)
    )
    received = lax.all_to_all(quant_out, "ep", split_axis=1, concat_axis=0, tiled=True)
    total = received.shape[0]
    rank_selector = (hot_plan[:, None] == jnp.arange(total, dtype=jnp.int32)[None, :]).astype(
        jnp.bfloat16
    )
    hot_values = jnp.einsum(
        "je,edf->jdf", rank_selector, received, preferred_element_type=jnp.float32
    ).astype(jnp.bfloat16)
    all_scales = lax.all_gather(scale_out, "ep", axis=0, tiled=True)
    every = all_scales.shape[0]
    scale_select = (hot_plan[:, None] == jnp.arange(every, dtype=jnp.int32)[None, :]).astype(
        jnp.float32
    )
    replica_block_scales = jnp.einsum(
        "je,ebc->jbc", scale_select, all_scales, precision=lax.Precision.HIGHEST
    )
    return (quant_out, scale_out, hot_values, replica_block_scales)


def solution(mesh):
    n, reps = mesh.shape["ep"], mesh.shape["rep"]

    placed = (
        P("ep", "rep", None),
        P("ep", "rep", None),
        P("ep", None, "rep"),
        P("ep", "rep", None),
        P(),
        P(),
        P(),
    )
    outs = (
        P("ep", "rep", None),
        P("ep", "rep", None),
        P(None, ("rep", "ep"), None),
        P(None, "rep", None),
    )

    def run(quant_in, scale_in, b_train, a_train, adapter_ranks, trainer_map, hot_plan):
        shapes = [v.shape for v in (quant_in, scale_in, b_train, a_train)]
        local = functools.partial(kernel_body, n, reps) if fits(n, reps, *shapes) else body
        step = jax.shard_map(local, mesh=mesh, in_specs=placed, out_specs=outs, check_vma=False)
        return step(quant_in, scale_in, b_train, a_train, adapter_ranks, trainer_map, hot_plan)

    return run
```

```python
import functools
import itertools
import math

import jax
import jax.numpy as jnp
from jax import lax
from jax.experimental import pallas as pl
from jax.experimental.pallas import tpu as pltpu
from jax.sharding import PartitionSpec as P

BLOCK = 128
RMAX = 64


EPS = 1e-06
MAX_PLANS = 128
MESH = pl.DeviceIdType.MESH


def exchange_kernel(n, reps, pieces, wide, cols, inv, b_ref, a_ref, bt_out, a_out,
                    b_mid, a_mid, b_stage, a_stage,
                    sb1, rb1, sa1, ra1, sb2, rb2, sa2, ra2):
    ep = lax.axis_index("ep")
    rep = lax.axis_index("rep")
    slab = pieces * wide
    barrier = pltpu.get_barrier_semaphore()
    for de in range(n):
        for dr in range(reps):
            if de or dr:
                pl.semaphore_signal(
                    barrier,
                    inc=1,
                    device_id={"ep": lax.rem(ep + de, n), "rep": lax.rem(rep + dr, reps)},
                    device_id_type=MESH,
                )
    pl.semaphore_wait(barrier, n * reps - 1)

    def move(own, src, dst, send, recv, de, dr):
        if own:
            return pltpu.make_async_copy(src, dst, recv)
        return pltpu.make_async_remote_copy(
            src_ref=src,
            dst_ref=dst,
            send_sem=send,
            recv_sem=recv,
            device_id={"ep": lax.rem(ep + de, n), "rep": lax.rem(rep + dr, reps)},
            device_id_type=MESH,
        )

    def b_first(de, dr):
        j, q = lax.rem(ep + de, n), lax.rem(rep + dr, reps)
        at = q * slab + jnp.minimum(j, pieces - 1) * wide
        src = b_ref.at[0, :, pl.ds(pl.multiple_of(at, BLOCK), wide)]
        return j, move(not (de or dr), src, b_mid.at[ep, rep], sb1.at[de, dr], rb1.at[ep, rep], de, dr)

    def a_first(de):
        j = lax.rem(ep + de, n)
        src = a_ref.at[0, :, pl.ds(pl.multiple_of(j * cols, cols), cols)]
        return move(de == 0, src, a_mid.at[ep], sa1.at[de], ra1.at[ep], de, 0)

    order = [(de, dr) for de in reversed(range(n)) for dr in range(reps)]
    for de in reversed(range(n)):
        a_first(de).start()
    for de, dr in order:
        j, copy = b_first(de, dr)
        pl.when(j < pieces)(copy.start)

    for s in range(n):
        pltpu.make_async_copy(a_mid.at[s], a_mid.at[s], ra1.at[s]).wait()
    for d in range(n):
        a_stage[d] = a_mid[inv[d]]

    def a_second(de, dr):
        d = lax.rem(ep + de, n)
        dst = a_out.at[rep, :, pl.ds(pl.multiple_of(ep * cols, cols), cols)]
        return move(not (de or dr), a_stage.at[d], dst, sa2.at[de, dr], ra2.at[ep, rep], de, dr)

    def b_second(de):
        d = lax.rem(ep + de, n)
        here = jnp.minimum(ep, pieces - 1)
        dst = bt_out.at[:, :, pl.ds(pl.multiple_of(here * wide, wide), wide)]
        return move(de == 0, b_stage.at[d], dst, sb2.at[de], rb2.at[ep], de, 0)

    for de, dr in order:
        a_second(de, dr).start()

    @pl.when(ep < pieces)
    def _():
        for s in range(n):
            for r in range(reps):
                pltpu.make_async_copy(b_mid.at[s, r], b_mid.at[s, r], rb1.at[s, r]).wait()
        for d in range(n):
            b_stage[d] = b_mid[inv[d]]
        for de in reversed(range(n)):
            b_second(de).start()

    for j in range(n):
        for q in range(reps):
            dst = a_out.at[q, :, pl.ds(j * cols, cols)]
            pltpu.make_async_copy(dst, dst, ra2.at[j, q]).wait()
    for j in range(pieces):
        dst = bt_out.at[:, :, pl.ds(j * wide, wide)]
        pltpu.make_async_copy(dst, dst, rb2.at[j]).wait()
    for de, dr in order:
        if de or dr:
            j, copy = b_first(de, dr)
            pl.when(j < pieces)(copy.wait_send)
            a_second(de, dr).wait_send()
    for de in range(1, n):
        a_first(de).wait_send()
        copy = b_second(de)
        pl.when(ep < pieces)(copy.wait_send)


def exchange(inv, b_train, a_train, n, reps):
    depth, ranks = b_train.shape[1:]
    features = a_train.shape[2]
    slab = depth // reps
    blocks = slab // BLOCK
    wide = -(-blocks // n) * BLOCK
    pieces = slab // wide
    cols = features // n
    bf16 = jnp.bfloat16
    dma = pltpu.SemaphoreType.DMA
    return pl.pallas_call(
        functools.partial(exchange_kernel, n, reps, pieces, wide, cols),
        out_shape=(
            jax.ShapeDtypeStruct((reps, ranks, slab), bf16),
            jax.ShapeDtypeStruct((reps, ranks, features), bf16),
        ),
        in_specs=[
            pl.BlockSpec(memory_space=pltpu.SMEM),
            pl.BlockSpec(memory_space=pltpu.VMEM),
            pl.BlockSpec(memory_space=pltpu.VMEM),
        ],
        out_specs=(pl.BlockSpec(memory_space=pltpu.VMEM),) * 2,
        scratch_shapes=[
            pltpu.VMEM((n, reps, ranks, wide), bf16),
            pltpu.VMEM((n, ranks, cols), bf16),
            pltpu.VMEM((n, reps, ranks, wide), bf16),
            pltpu.VMEM((n, ranks, cols), bf16),
            dma((n, reps)), dma((n, reps)), dma((n,)), dma((n,)),
            dma((n,)), dma((n,)), dma((n, reps)), dma((n, reps)),
        ],
        compiler_params=pltpu.CompilerParams(
            collective_id=0, has_side_effects=True, vmem_limit_bytes=32 << 20
        ),
        name="exchange",
    )(inv, jnp.swapaxes(b_train, 1, 2), a_train)


def merge_kernel(rank, scale_in, quant_in, bt, a, quant_out, scale_out, live):
    step = pl.program_id(0)
    blocks = quant_in.shape[1] // BLOCK
    col_blocks = quant_in.shape[2] // BLOCK

    @pl.when(step == 0)
    def _():
        keep = lax.broadcasted_iota(jnp.int32, live.shape, 0) < rank[0]
        live[...] = jnp.where(keep, a[...].astype(jnp.float32), 0.0).astype(jnp.bfloat16)

    lane = lax.broadcasted_iota(jnp.int32, (1, col_blocks), 1)
    for i in range(blocks):
        delta = lax.dot_general(
            bt[:, i * BLOCK:(i + 1) * BLOCK], live[...], (((0,), (0,)), ((), ())),
            preferred_element_type=jnp.float32,
        )
        rows = slice(i * BLOCK, (i + 1) * BLOCK)
        found = jnp.zeros((1, col_blocks), jnp.float32)
        for c in range(col_blocks):
            cut = slice(c * BLOCK, (c + 1) * BLOCK)
            held = quant_in[0, rows, cut].astype(jnp.float32)
            merged = held * scale_in[0, step * blocks + i, c] + delta[:, cut]
            top = jnp.max(jnp.max(jnp.abs(merged), axis=0, keepdims=True), axis=1, keepdims=True) + EPS
            quant_out[0, rows, cut] = (merged * (1.0 / top)).astype(jnp.bfloat16)
            found = jnp.where(lane == c, top, found)
        scale_out[0, pl.ds(step * blocks + i, 1), :] = found


def merge(rank, scale_in, quant_in, bt, a):
    _, rows, features = quant_in.shape
    total = rows // BLOCK
    blocks = 2 if total % 2 == 0 else 1
    steps = total // blocks
    tall = blocks * BLOCK
    return pl.pallas_call(
        merge_kernel,
        grid=(steps,),
        out_shape=(
            jax.ShapeDtypeStruct(quant_in.shape, jnp.bfloat16),
            jax.ShapeDtypeStruct(scale_in.shape, jnp.float32),
        ),
        in_specs=[
            pl.BlockSpec(memory_space=pltpu.SMEM),
            pl.BlockSpec(memory_space=pltpu.SMEM),
            pl.BlockSpec((1, tall, features), lambda i: (0, i, 0)),
            pl.BlockSpec((bt.shape[0], tall), lambda i: (0, i)),
            pl.BlockSpec(a.shape, lambda i: (0, 0)),
        ],
        out_specs=(
            pl.BlockSpec((1, tall, features), lambda i: (0, i, 0)),
            pl.BlockSpec(scale_in.shape, lambda i: (0, 0, 0)),
        ),
        scratch_shapes=[pltpu.VMEM(a.shape, jnp.bfloat16)],
        compiler_params=pltpu.CompilerParams(vmem_limit_bytes=32 << 20),
        name="merge",
    )(rank, scale_in, quant_in, bt, a)


def hot_kernel(n, sources, piece, chunks, quant, scale, slots, scales, hold,
               send, recv, forward_send, hold_recv, scale_send, scale_recv):
    ep = lax.axis_index("ep")
    line = lax.rem(ep, 2)
    spot = lax.div(ep, 2)
    half = n // 2
    partner = ep + 1 - 2 * line
    size = piece // chunks

    def source(e):
        hit = functools.reduce(jnp.logical_or, [e == s for s in sources])
        slot = sum((e > s).astype(jnp.int32) for s in sources)
        return hit, jnp.minimum(slot, len(sources) - 1)

    mine, slot = source(ep)
    theirs, partner_slot = source(partner)

    def at(de):
        return {"ep": lax.rem(ep + de, n)}

    barrier = pltpu.get_barrier_semaphore()

    @pl.loop(1, n)
    def _(de):
        pl.semaphore_signal(barrier, inc=1, device_id=at(de), device_id_type=MESH)

    pl.semaphore_wait(barrier, n - 1)

    def remote(src, dst, send_sem, recv_sem, p):
        return pltpu.make_async_remote_copy(
            src_ref=src, dst_ref=dst, send_sem=send_sem, recv_sem=recv_sem,
            device_id={"ep": p}, device_id_type=MESH,
        )

    def far(i):
        if half == 4:
            step = 2 if i == 0 else (3 - 2 * lax.rem(spot, 2) if i == 1 else 1 + 2 * lax.rem(spot, 2))
        else:
            step = i + 1
        return lax.rem(spot + step, half)

    def piece_rows(p):
        return quant.at[0, pl.ds(pl.multiple_of(p * piece, 16), piece)]

    def chunk(c):
        return pl.ds(pl.multiple_of(c * size, 16), size)

    def direct(p, sem):
        return remote(piece_rows(p), slots.at[slot], send.at[sem], recv.at[slot], p)

    def along(i):
        return direct(far(i) * 2 + line, i)

    def lend(i, c):
        p = far(i) * 2 + 1 - line
        rows = pl.ds(pl.multiple_of(p * piece + c * size, 16), size)
        return remote(
            quant.at[0, rows], hold.at[i, chunk(c)], send.at[half + i], hold_recv.at[i, c], partner
        )

    def forward(i, c):
        return remote(
            hold.at[i, chunk(c)], slots.at[partner_slot, chunk(c)], forward_send.at[i],
            recv.at[partner_slot], far(i) * 2 + line,
        )

    def scale_copy(de):
        return pltpu.make_async_remote_copy(
            src_ref=scale, dst_ref=scales.at[pl.ds(ep, 1)], send_sem=scale_send.at[de],
            recv_sem=scale_recv.at[ep], device_id=at(de), device_id_type=MESH,
        )

    own = pltpu.make_async_copy(piece_rows(ep), slots.at[slot], recv.at[slot])

    @pl.when(mine)
    def _():
        for i in range(half - 1):
            @pl.loop(0, chunks)
            def _(c):
                lend(i, c).start()

            along(i).start()
        direct(partner, half - 1).start()
        own.start()

    pltpu.make_async_copy(scale, scales.at[pl.ds(ep, 1)], scale_recv.at[ep]).start()

    @pl.loop(1, n)
    def _(de):
        scale_copy(de).start()

    @pl.when(theirs)
    def _():
        for i in range(half - 1):
            @pl.loop(0, chunks)
            def _(c):
                pltpu.make_async_copy(
                    hold.at[i, chunk(c)], hold.at[i, chunk(c)], hold_recv.at[i, c]
                ).wait()
                forward(i, c).start()

    @pl.loop(0, n)
    def _(s):
        pltpu.make_async_copy(scales.at[pl.ds(s, 1)], scales.at[pl.ds(s, 1)], scale_recv.at[s]).wait()

    @pl.loop(1, n)
    def _(de):
        scale_copy(de).wait_send()

    @pl.loop(0, len(sources))
    def _(k):
        pltpu.make_async_copy(slots.at[k], slots.at[k], recv.at[k]).wait()

    @pl.when(theirs)
    def _():
        for i in range(half - 1):
            pltpu.make_async_copy(hold.at[i], hold.at[i], forward_send.at[i]).wait()

    @pl.when(mine)
    def _():
        for i in range(2 * half - 1):
            pltpu.make_async_copy(slots.at[slot], slots.at[slot], send.at[i]).wait()


def spread(quant, scale, n, sources, collective_id):
    piece = quant.shape[1] // n
    chunks = next(c for c in (7, 5, 4, 3, 2, 1) if piece % (16 * c) == 0)
    half = n // 2
    dma = pltpu.SemaphoreType.DMA
    return pl.pallas_call(
        functools.partial(hot_kernel, n, sources, piece, chunks),
        out_shape=(
            jax.ShapeDtypeStruct((len(sources), piece, quant.shape[2]), quant.dtype),
            jax.ShapeDtypeStruct((n,) + scale.shape[1:], scale.dtype),
            jax.ShapeDtypeStruct((half - 1, piece, quant.shape[2]), quant.dtype),
        ),
        in_specs=[
            pl.BlockSpec(memory_space=pl.ANY),
            pl.BlockSpec(memory_space=pltpu.VMEM),
        ],
        out_specs=(
            pl.BlockSpec(memory_space=pl.ANY),
            pl.BlockSpec(memory_space=pltpu.VMEM),
            pl.BlockSpec(memory_space=pl.ANY),
        ),
        scratch_shapes=[
            dma((2 * half,)), dma((len(sources),)), dma((half,)), dma((half, chunks)),
            dma((n,)), dma((n,)),
        ],
        compiler_params=pltpu.CompilerParams(collective_id=collective_id, has_side_effects=True),
        name="spread",
    )(quant, scale)[:2]


def place_kernel(where, plan, held, scales, values, picked):
    values[...] = held[...]

    @pl.when(pl.program_id(0) == 0)
    def _():
        for k in range(picked.shape[0]):
            picked[k] = scales[plan[k]]


def place(where, plan, slots, scales):
    count = plan.shape[0]
    block = (1,) + slots.shape[1:]
    return pl.pallas_call(
        place_kernel,
        grid_spec=pltpu.PrefetchScalarGridSpec(
            num_scalar_prefetch=2,
            grid=(count,),
            in_specs=[
                pl.BlockSpec(block, lambda k, where, plan: (where[k], 0, 0)),
                pl.BlockSpec(scales.shape, lambda k, where, plan: (0, 0, 0)),
            ],
            out_specs=[
                pl.BlockSpec(block, lambda k, where, plan: (k, 0, 0)),
                pl.BlockSpec((count,) + scales.shape[1:], lambda k, where, plan: (0, 0, 0)),
            ],
        ),
        out_shape=(
            jax.ShapeDtypeStruct((count,) + slots.shape[1:], slots.dtype),
            jax.ShapeDtypeStruct((count,) + scales.shape[1:], scales.dtype),
        ),
        compiler_params=pltpu.CompilerParams(vmem_limit_bytes=32 << 20),
        name="place",
    )(where, plan, slots, scales)


def kernel_body(n, reps, quant_in, scale_in, b_train, a_train, adapter_ranks, trainer_map, hot_plan):
    owner = lax.axis_index("ep")
    serving = jnp.arange(n, dtype=jnp.int32)
    inv = jnp.sum(
        jnp.where(trainer_map[None, :] == serving[:, None], serving[None, :], 0), axis=1
    ).astype(jnp.int32)
    bt, a = exchange(inv, b_train, a_train, n, reps)
    bt = bt.reshape(-1, bt.shape[2])
    a = a.reshape(-1, a.shape[2])
    rank = lax.dynamic_slice_in_dim(adapter_ranks, owner, 1, 0)
    quant_out, scale_out = merge(rank, scale_in, quant_in, bt, a)
    count = hot_plan.shape[0]
    plans = list(itertools.combinations(range(n), count))
    if len(plans) <= MAX_PLANS:
        table = [0] * (1 << n)
        for at, chosen in enumerate(plans):
            table[sum(1 << e for e in chosen)] = at
        which = jnp.asarray(table, jnp.int32)[jnp.sum(jnp.left_shift(1, hot_plan))]
        branches = [
            functools.partial(spread, n=n, sources=chosen, collective_id=1 + at)
            for at, chosen in enumerate(plans)
        ]
        slots, scales = lax.switch(which, branches, quant_out, scale_out)
        where = jnp.sum((hot_plan[None, :] < hot_plan[:, None]).astype(jnp.int32), axis=1)
    else:
        slots, scales = spread(quant_out, scale_out, n, tuple(range(n)), 1)
        where = hot_plan
    hot_values, replica_block_scales = place(where.astype(jnp.int32), hot_plan, slots, scales)
    return quant_out, scale_out, hot_values, replica_block_scales


def fits(n, reps, quant_in, scale_in, b_train, a_train):
    slab = b_train[1] // reps
    blocks = slab // BLOCK
    wide = -(-blocks // n)
    return (
        quant_in[0] == n
        and n % 2 == 0
        and n > 2
        and blocks * BLOCK == slab
        and blocks % wide == 0
        and (b_train[2] // reps) % 16 == 0
        and a_train[2] % (n * BLOCK) == 0
        and (slab // n) % 16 == 0
    )


def body(quant_in, scale_in, b_train, a_train, adapter_ranks, trainer_map, hot_plan):
    exp_dev = quant_in.shape[0]
    rows = quant_in.shape[1]
    cols = quant_in.shape[2]
    owner = lax.axis_index("ep")
    owned_expert_index = owner * exp_dev + jnp.arange(exp_dev, dtype=jnp.int32)
    b_rows = lax.all_to_all(b_train, "rep", split_axis=1, concat_axis=2, tiled=True)
    a_full = lax.all_gather(a_train, "rep", axis=1, tiled=True)
    rank_selector = (trainer_map[None, :] == owned_expert_index[:, None]).astype(jnp.bfloat16)
    b_sum = jnp.einsum(
        "ji,idr->jdr",
        rank_selector,
        lax.all_gather(b_rows, "ep", axis=0, tiled=True),
        preferred_element_type=jnp.float32,
    )
    a_sum = jnp.einsum(
        "ji,irf->jrf",
        rank_selector,
        lax.all_gather(a_full, "ep", axis=0, tiled=True),
        preferred_element_type=jnp.float32,
    )
    serving_up_factor = b_sum.astype(jnp.bfloat16)
    a_serv = a_sum.astype(jnp.bfloat16)
    local_rank_indices = lax.dynamic_slice_in_dim(adapter_ranks, owner * exp_dev, exp_dev, 0)
    live = (jnp.arange(RMAX, dtype=jnp.int32)[None, :] < local_rank_indices[:, None]).astype(
        jnp.bfloat16
    )
    active_down_factor = a_serv * live[:, :, None]
    weight_update = jnp.einsum(
        "enw,ewk->enk", serving_up_factor, active_down_factor, preferred_element_type=jnp.float32
    )
    row_blocks = rows // BLOCK
    col_blocks = cols // BLOCK
    expert_weight_tensor = (
        quant_in.astype(jnp.float32).reshape(exp_dev, row_blocks, BLOCK, col_blocks, BLOCK)
        * scale_in[:, :, None, :, None]
    )
    merged = expert_weight_tensor + weight_update.reshape(
        exp_dev, row_blocks, BLOCK, col_blocks, BLOCK
    )
    scale_out = jnp.max(jnp.abs(merged), axis=(2, 4)) + EPS
    quant_out = (
        (merged / scale_out[:, :, None, :, None]).reshape(exp_dev, rows, cols).astype(jnp.bfloat16)
    )
    received = lax.all_to_all(quant_out, "ep", split_axis=1, concat_axis=0, tiled=True)
    total = received.shape[0]
    rank_selector = (hot_plan[:, None] == jnp.arange(total, dtype=jnp.int32)[None, :]).astype(
        jnp.bfloat16
    )
    hot_values = jnp.einsum(
        "je,edf->jdf", rank_selector, received, preferred_element_type=jnp.float32
    ).astype(jnp.bfloat16)
    all_scales = lax.all_gather(scale_out, "ep", axis=0, tiled=True)
    every = all_scales.shape[0]
    scale_select = (hot_plan[:, None] == jnp.arange(every, dtype=jnp.int32)[None, :]).astype(
        jnp.float32
    )
    replica_block_scales = jnp.einsum(
        "je,ebc->jbc", scale_select, all_scales, precision=lax.Precision.HIGHEST
    )
    return (quant_out, scale_out, hot_values, replica_block_scales)


def solution(mesh):
    n, reps = mesh.shape["ep"], mesh.shape["rep"]

    placed = (
        P("ep", "rep", None),
        P("ep", "rep", None),
        P("ep", None, "rep"),
        P("ep", "rep", None),
        P(),
        P(),
        P(),
    )
    outs = (
        P("ep", "rep", None),
        P("ep", "rep", None),
        P(None, ("rep", "ep"), None),
        P(None, "rep", None),
    )

    def run(quant_in, scale_in, b_train, a_train, adapter_ranks, trainer_map, hot_plan):
        shapes = [v.shape for v in (quant_in, scale_in, b_train, a_train)]
        local = functools.partial(kernel_body, n, reps) if fits(n, reps, *shapes) else body
        step = jax.shard_map(local, mesh=mesh, in_specs=placed, out_specs=outs, check_vma=False)
        return step(quant_in, scale_in, b_train, a_train, adapter_ranks, trainer_map, hot_plan)

    return run
```

```python
import functools
import itertools
import math

import jax
import jax.numpy as jnp
from jax import lax
from jax.experimental import pallas as pl
from jax.experimental.pallas import tpu as pltpu
from jax.sharding import PartitionSpec as P

BLOCK = 128
RMAX = 64


EPS = 1e-06
MAX_PLANS = 128
MESH = pl.DeviceIdType.MESH


def exchange_kernel(n, reps, pieces, wide, cols, inv, b_ref, a_ref, bt_out, a_out,
                    b_mid, a_mid, b_stage, a_stage,
                    sb1, rb1, sa1, ra1, sb2, rb2, sa2, ra2, sa3, ra3):
    ep = lax.axis_index("ep")
    rep = lax.axis_index("rep")
    slab = pieces * wide
    barrier = pltpu.get_barrier_semaphore()
    for de in range(n):
        for dr in range(reps):
            if de or dr:
                pl.semaphore_signal(
                    barrier,
                    inc=1,
                    device_id={"ep": lax.rem(ep + de, n), "rep": lax.rem(rep + dr, reps)},
                    device_id_type=MESH,
                )
    pl.semaphore_wait(barrier, n * reps - 1)

    def move(own, src, dst, send, recv, de, dr):
        if own:
            return pltpu.make_async_copy(src, dst, recv)
        return pltpu.make_async_remote_copy(
            src_ref=src,
            dst_ref=dst,
            send_sem=send,
            recv_sem=recv,
            device_id={"ep": lax.rem(ep + de, n), "rep": lax.rem(rep + dr, reps)},
            device_id_type=MESH,
        )

    def b_first(de, dr):
        j, q = lax.rem(ep + de, n), lax.rem(rep + dr, reps)
        at = q * slab + jnp.minimum(j, pieces - 1) * wide
        src = b_ref.at[0, :, pl.ds(pl.multiple_of(at, BLOCK), wide)]
        return j, move(not (de or dr), src, b_mid.at[ep, rep], sb1.at[de, dr], rb1.at[ep, rep], de, dr)

    def a_first(de):
        j = lax.rem(ep + de, n)
        src = a_ref.at[0, :, pl.ds(pl.multiple_of(j * cols, cols), cols)]
        return move(de == 0, src, a_mid.at[ep], sa1.at[de], ra1.at[ep], de, 0)

    order = [(de, dr) for de in reversed(range(n)) for dr in range(reps)]
    for de in reversed(range(n)):
        a_first(de).start()
    for de, dr in order:
        j, copy = b_first(de, dr)
        pl.when(j < pieces)(copy.start)

    for s in range(n):
        pltpu.make_async_copy(a_mid.at[s], a_mid.at[s], ra1.at[s]).wait()
    for d in range(n):
        a_stage[d] = a_mid[inv[d]]

    def a_second(de):
        d = lax.rem(ep + de, n)
        dst = a_out.at[rep, :, pl.ds(pl.multiple_of(ep * cols, cols), cols)]
        return move(de == 0, a_stage.at[d], dst, sa2.at[de], ra2.at[ep], de, 0)

    def a_third(dr):
        return move(False, a_out.at[rep], a_out.at[rep], sa3.at[dr], ra3.at[rep], 0, dr)

    def b_second(de):
        d = lax.rem(ep + de, n)
        here = jnp.minimum(ep, pieces - 1)
        dst = bt_out.at[:, :, pl.ds(pl.multiple_of(here * wide, wide), wide)]
        return move(de == 0, b_stage.at[d], dst, sb2.at[de], rb2.at[ep], de, 0)

    for de in reversed(range(n)):
        a_second(de).start()

    @pl.when(ep < pieces)
    def _():
        for s in range(n):
            for r in range(reps):
                pltpu.make_async_copy(b_mid.at[s, r], b_mid.at[s, r], rb1.at[s, r]).wait()
        for d in range(n):
            b_stage[d] = b_mid[inv[d]]
        for de in reversed(range(n)):
            b_second(de).start()

    for j in range(n):
        dst = a_out.at[rep, :, pl.ds(j * cols, cols)]
        pltpu.make_async_copy(dst, dst, ra2.at[j]).wait()
    for dr in range(1, reps):
        a_third(dr).start()
    for dr in range(1, reps):
        q = lax.rem(rep + dr, reps)
        pltpu.make_async_copy(a_out.at[q], a_out.at[q], ra3.at[q]).wait()
    for j in range(pieces):
        dst = bt_out.at[:, :, pl.ds(j * wide, wide)]
        pltpu.make_async_copy(dst, dst, rb2.at[j]).wait()
    for de, dr in order:
        if de or dr:
            j, copy = b_first(de, dr)
            pl.when(j < pieces)(copy.wait_send)
    for dr in range(1, reps):
        a_third(dr).wait_send()
    for de in range(1, n):
        a_first(de).wait_send()
        a_second(de).wait_send()
        copy = b_second(de)
        pl.when(ep < pieces)(copy.wait_send)


def exchange(inv, b_train, a_train, n, reps):
    depth, ranks = b_train.shape[1:]
    features = a_train.shape[2]
    slab = depth // reps
    blocks = slab // BLOCK
    wide = -(-blocks // n) * BLOCK
    pieces = slab // wide
    cols = features // n
    bf16 = jnp.bfloat16
    dma = pltpu.SemaphoreType.DMA
    return pl.pallas_call(
        functools.partial(exchange_kernel, n, reps, pieces, wide, cols),
        out_shape=(
            jax.ShapeDtypeStruct((reps, ranks, slab), bf16),
            jax.ShapeDtypeStruct((reps, ranks, features), bf16),
        ),
        in_specs=[
            pl.BlockSpec(memory_space=pltpu.SMEM),
            pl.BlockSpec(memory_space=pl.ANY),
            pl.BlockSpec(memory_space=pl.ANY),
        ],
        out_specs=(pl.BlockSpec(memory_space=pltpu.VMEM),) * 2,
        scratch_shapes=[
            pltpu.VMEM((n, reps, ranks, wide), bf16),
            pltpu.VMEM((n, ranks, cols), bf16),
            pltpu.VMEM((n, reps, ranks, wide), bf16),
            pltpu.VMEM((n, ranks, cols), bf16),
            dma((n, reps)), dma((n, reps)), dma((n,)), dma((n,)),
            dma((n,)), dma((n,)), dma((n,)), dma((n,)), dma((reps,)), dma((reps,)),
        ],
        compiler_params=pltpu.CompilerParams(
            collective_id=0, has_side_effects=True
        ),
        name="exchange",
    )(inv, jnp.swapaxes(b_train, 1, 2), a_train)


def merge_kernel(ranks, scale_in, quant_in, bt, a, quant_out, scale_out, live):
    step = pl.program_id(0)
    blocks = quant_in.shape[1] // BLOCK
    col_blocks = quant_in.shape[2] // BLOCK

    @pl.when(step == 0)
    def _():
        keep = lax.broadcasted_iota(jnp.int32, live.shape, 0) < ranks[lax.axis_index("ep")]
        live[...] = jnp.where(keep, a[...].astype(jnp.float32), 0.0).astype(jnp.bfloat16)

    lane = lax.broadcasted_iota(jnp.int32, (1, col_blocks), 1)
    for i in range(blocks):
        delta = lax.dot_general(
            bt[:, i * BLOCK:(i + 1) * BLOCK], live[...], (((0,), (0,)), ((), ())),
            preferred_element_type=jnp.float32,
        )
        rows = slice(i * BLOCK, (i + 1) * BLOCK)
        found = jnp.zeros((1, col_blocks), jnp.float32)
        for c in range(col_blocks):
            cut = slice(c * BLOCK, (c + 1) * BLOCK)
            held = quant_in[0, rows, cut].astype(jnp.float32)
            merged = held * scale_in[0, step * blocks + i, c] + delta[:, cut]
            top = jnp.max(jnp.max(jnp.abs(merged), axis=0, keepdims=True), axis=1, keepdims=True) + EPS
            quant_out[0, rows, cut] = (merged * (1.0 / top)).astype(jnp.bfloat16)
            found = jnp.where(lane == c, top, found)
        scale_out[0, pl.ds(step * blocks + i, 1), :] = found


def merge(ranks, scale_in, quant_in, bt, a):
    _, rows, features = quant_in.shape
    total = rows // BLOCK
    blocks = 2 if total % 2 == 0 else 1
    steps = total // blocks
    tall = blocks * BLOCK
    return pl.pallas_call(
        merge_kernel,
        grid=(steps,),
        out_shape=(
            jax.ShapeDtypeStruct(quant_in.shape, jnp.bfloat16),
            jax.ShapeDtypeStruct(scale_in.shape, jnp.float32),
        ),
        in_specs=[
            pl.BlockSpec(memory_space=pltpu.SMEM),
            pl.BlockSpec(memory_space=pltpu.SMEM),
            pl.BlockSpec((1, tall, features), lambda i: (0, i, 0)),
            pl.BlockSpec((bt.shape[0], tall), lambda i: (0, i)),
            pl.BlockSpec(a.shape, lambda i: (0, 0)),
        ],
        out_specs=(
            pl.BlockSpec((1, tall, features), lambda i: (0, i, 0)),
            pl.BlockSpec(scale_in.shape, lambda i: (0, 0, 0)),
        ),
        scratch_shapes=[pltpu.VMEM(a.shape, jnp.bfloat16)],
        name="merge",
    )(ranks, scale_in, quant_in, bt, a)


def hot_kernel(n, sources, piece, chunks, quant, scale, slots, scales, hold,
               send, recv, forward_send, hold_recv, scale_send, scale_recv):
    ep = lax.axis_index("ep")
    line = lax.rem(ep, 2)
    spot = lax.div(ep, 2)
    half = n // 2
    partner = ep + 1 - 2 * line
    size = piece // chunks

    def source(e):
        hit = functools.reduce(jnp.logical_or, [e == s for s in sources])
        slot = sum((e > s).astype(jnp.int32) for s in sources)
        return hit, jnp.minimum(slot, len(sources) - 1)

    mine, slot = source(ep)
    theirs, partner_slot = source(partner)

    def at(de):
        return {"ep": lax.rem(ep + de, n)}

    barrier = pltpu.get_barrier_semaphore()

    @pl.loop(1, n)
    def _(de):
        pl.semaphore_signal(barrier, inc=1, device_id=at(de), device_id_type=MESH)

    pl.semaphore_wait(barrier, n - 1)

    def remote(src, dst, send_sem, recv_sem, p):
        return pltpu.make_async_remote_copy(
            src_ref=src, dst_ref=dst, send_sem=send_sem, recv_sem=recv_sem,
            device_id={"ep": p}, device_id_type=MESH,
        )

    def far(i):
        if half == 4:
            step = 2 if i == 0 else (3 - 2 * lax.rem(spot, 2) if i == 1 else 1 + 2 * lax.rem(spot, 2))
        else:
            step = i + 1
        return lax.rem(spot + step, half)

    def piece_rows(p):
        return quant.at[0, pl.ds(pl.multiple_of(p * piece, 16), piece)]

    def chunk(c):
        return pl.ds(pl.multiple_of(c * size, 16), size)

    def direct(p, sem):
        return remote(piece_rows(p), slots.at[slot], send.at[sem], recv.at[slot], p)

    def along(i):
        return direct(far(i) * 2 + line, i)

    def lend(i, c):
        p = far(i) * 2 + 1 - line
        rows = pl.ds(pl.multiple_of(p * piece + c * size, 16), size)
        return remote(
            quant.at[0, rows], hold.at[i, chunk(c)], send.at[half + i], hold_recv.at[i, c], partner
        )

    def forward(i, c):
        return remote(
            hold.at[i, chunk(c)], slots.at[partner_slot, chunk(c)], forward_send.at[i],
            recv.at[partner_slot], far(i) * 2 + line,
        )

    def scale_copy(de):
        return pltpu.make_async_remote_copy(
            src_ref=scale, dst_ref=scales.at[pl.ds(ep, 1)], send_sem=scale_send.at[de],
            recv_sem=scale_recv.at[ep], device_id=at(de), device_id_type=MESH,
        )

    own = pltpu.make_async_copy(piece_rows(ep), slots.at[slot], recv.at[slot])

    @pl.when(mine)
    def _():
        for i in range(half - 1):
            @pl.loop(0, chunks)
            def _(c):
                lend(i, c).start()

            along(i).start()
        direct(partner, half - 1).start()
        own.start()

    pltpu.make_async_copy(scale, scales.at[pl.ds(ep, 1)], scale_recv.at[ep]).start()

    @pl.loop(1, n)
    def _(de):
        scale_copy(de).start()

    @pl.when(theirs)
    def _():
        for i in range(half - 1):
            @pl.loop(0, chunks)
            def _(c):
                pltpu.make_async_copy(
                    hold.at[i, chunk(c)], hold.at[i, chunk(c)], hold_recv.at[i, c]
                ).wait()
                forward(i, c).start()

    @pl.loop(0, n)
    def _(s):
        pltpu.make_async_copy(scales.at[pl.ds(s, 1)], scales.at[pl.ds(s, 1)], scale_recv.at[s]).wait()

    @pl.loop(1, n)
    def _(de):
        scale_copy(de).wait_send()

    @pl.loop(0, len(sources))
    def _(k):
        pltpu.make_async_copy(slots.at[k], slots.at[k], recv.at[k]).wait()

    @pl.when(theirs)
    def _():
        for i in range(half - 1):
            pltpu.make_async_copy(hold.at[i], hold.at[i], forward_send.at[i]).wait()

    @pl.when(mine)
    def _():
        for i in range(2 * half - 1):
            pltpu.make_async_copy(slots.at[slot], slots.at[slot], send.at[i]).wait()


def spread(quant, scale, n, sources, collective_id):
    piece = quant.shape[1] // n
    chunks = next(c for c in (7, 5, 4, 3, 2, 1) if piece % (16 * c) == 0)
    half = n // 2
    dma = pltpu.SemaphoreType.DMA
    return pl.pallas_call(
        functools.partial(hot_kernel, n, sources, piece, chunks),
        out_shape=(
            jax.ShapeDtypeStruct((len(sources), piece, quant.shape[2]), quant.dtype),
            jax.ShapeDtypeStruct((n,) + scale.shape[1:], scale.dtype),
            jax.ShapeDtypeStruct((half - 1, piece, quant.shape[2]), quant.dtype),
        ),
        in_specs=[
            pl.BlockSpec(memory_space=pl.ANY),
            pl.BlockSpec(memory_space=pltpu.VMEM),
        ],
        out_specs=(
            pl.BlockSpec(memory_space=pl.ANY),
            pl.BlockSpec(memory_space=pltpu.VMEM),
            pl.BlockSpec(memory_space=pl.ANY),
        ),
        scratch_shapes=[
            dma((2 * half,)), dma((len(sources),)), dma((half,)), dma((half, chunks)),
            dma((n,)), dma((n,)),
        ],
        compiler_params=pltpu.CompilerParams(collective_id=collective_id, has_side_effects=True),
        name="spread",
    )(quant, scale)[:2]


def place_kernel(where, plan, held, scales, values, picked):
    values[...] = held[...]

    @pl.when((pl.program_id(0) == 0) & (pl.program_id(1) == 0))
    def _():
        for k in range(picked.shape[0]):
            picked[k] = scales[plan[k]]


def place(where, plan, slots, scales):
    count = plan.shape[0]
    parts = 2
    block = (1, slots.shape[1] // parts, slots.shape[2])
    return pl.pallas_call(
        place_kernel,
        grid_spec=pltpu.PrefetchScalarGridSpec(
            num_scalar_prefetch=2,
            grid=(count, parts),
            in_specs=[
                pl.BlockSpec(block, lambda k, h, where, plan: (where[k], h, 0)),
                pl.BlockSpec(scales.shape, lambda k, h, where, plan: (0, 0, 0)),
            ],
            out_specs=[
                pl.BlockSpec(block, lambda k, h, where, plan: (k, h, 0)),
                pl.BlockSpec((count,) + scales.shape[1:], lambda k, h, where, plan: (0, 0, 0)),
            ],
        ),
        out_shape=(
            jax.ShapeDtypeStruct((count,) + slots.shape[1:], slots.dtype),
            jax.ShapeDtypeStruct((count,) + scales.shape[1:], scales.dtype),
        ),
        name="place",
    )(where, plan, slots, scales)


def kernel_body(n, reps, quant_in, scale_in, b_train, a_train, adapter_ranks, trainer_map, hot_plan):
    serving = jnp.arange(n, dtype=jnp.int32)
    inv = jnp.sum(
        jnp.where(trainer_map[None, :] == serving[:, None], serving[None, :], 0), axis=1
    ).astype(jnp.int32)
    bt, a = exchange(inv, b_train, a_train, n, reps)
    bt = bt.reshape(-1, bt.shape[2])
    a = a.reshape(-1, a.shape[2])
    quant_out, scale_out = merge(adapter_ranks, scale_in, quant_in, bt, a)
    count = hot_plan.shape[0]
    plans = list(itertools.combinations(range(n), count))
    if len(plans) <= MAX_PLANS:
        table = [0] * (1 << n)
        for at, chosen in enumerate(plans):
            table[sum(1 << e for e in chosen)] = at
        which = jnp.asarray(table, jnp.int32)[jnp.sum(jnp.left_shift(1, hot_plan))]
        branches = [
            functools.partial(spread, n=n, sources=chosen, collective_id=1 + at)
            for at, chosen in enumerate(plans)
        ]
        slots, scales = lax.switch(which, branches, quant_out, scale_out)
        where = jnp.sum((hot_plan[None, :] < hot_plan[:, None]).astype(jnp.int32), axis=1)
    else:
        slots, scales = spread(quant_out, scale_out, n, tuple(range(n)), 1)
        where = hot_plan
    hot_values, replica_block_scales = place(where.astype(jnp.int32), hot_plan, slots, scales)
    return quant_out, scale_out, hot_values, replica_block_scales


def fits(n, reps, quant_in, scale_in, b_train, a_train):
    slab = b_train[1] // reps
    blocks = slab // BLOCK
    wide = -(-blocks // n)
    return (
        quant_in[0] == n
        and n % 2 == 0
        and n > 2
        and blocks * BLOCK == slab
        and blocks % wide == 0
        and (b_train[2] // reps) % 16 == 0
        and a_train[2] % (n * BLOCK) == 0
        and (slab // n) % 32 == 0
    )


def body(quant_in, scale_in, b_train, a_train, adapter_ranks, trainer_map, hot_plan):
    exp_dev = quant_in.shape[0]
    rows = quant_in.shape[1]
    cols = quant_in.shape[2]
    owner = lax.axis_index("ep")
    owned_expert_index = owner * exp_dev + jnp.arange(exp_dev, dtype=jnp.int32)
    b_rows = lax.all_to_all(b_train, "rep", split_axis=1, concat_axis=2, tiled=True)
    a_full = lax.all_gather(a_train, "rep", axis=1, tiled=True)
    rank_selector = (trainer_map[None, :] == owned_expert_index[:, None]).astype(jnp.bfloat16)
    b_sum = jnp.einsum(
        "ji,idr->jdr",
        rank_selector,
        lax.all_gather(b_rows, "ep", axis=0, tiled=True),
        preferred_element_type=jnp.float32,
    )
    a_sum = jnp.einsum(
        "ji,irf->jrf",
        rank_selector,
        lax.all_gather(a_full, "ep", axis=0, tiled=True),
        preferred_element_type=jnp.float32,
    )
    serving_up_factor = b_sum.astype(jnp.bfloat16)
    a_serv = a_sum.astype(jnp.bfloat16)
    local_rank_indices = lax.dynamic_slice_in_dim(adapter_ranks, owner * exp_dev, exp_dev, 0)
    live = (jnp.arange(RMAX, dtype=jnp.int32)[None, :] < local_rank_indices[:, None]).astype(
        jnp.bfloat16
    )
    active_down_factor = a_serv * live[:, :, None]
    weight_update = jnp.einsum(
        "enw,ewk->enk", serving_up_factor, active_down_factor, preferred_element_type=jnp.float32
    )
    row_blocks = rows // BLOCK
    col_blocks = cols // BLOCK
    expert_weight_tensor = (
        quant_in.astype(jnp.float32).reshape(exp_dev, row_blocks, BLOCK, col_blocks, BLOCK)
        * scale_in[:, :, None, :, None]
    )
    merged = expert_weight_tensor + weight_update.reshape(
        exp_dev, row_blocks, BLOCK, col_blocks, BLOCK
    )
    scale_out = jnp.max(jnp.abs(merged), axis=(2, 4)) + EPS
    quant_out = (
        (merged / scale_out[:, :, None, :, None]).reshape(exp_dev, rows, cols).astype(jnp.bfloat16)
    )
    received = lax.all_to_all(quant_out, "ep", split_axis=1, concat_axis=0, tiled=True)
    total = received.shape[0]
    rank_selector = (hot_plan[:, None] == jnp.arange(total, dtype=jnp.int32)[None, :]).astype(
        jnp.bfloat16
    )
    hot_values = jnp.einsum(
        "je,edf->jdf", rank_selector, received, preferred_element_type=jnp.float32
    ).astype(jnp.bfloat16)
    all_scales = lax.all_gather(scale_out, "ep", axis=0, tiled=True)
    every = all_scales.shape[0]
    scale_select = (hot_plan[:, None] == jnp.arange(every, dtype=jnp.int32)[None, :]).astype(
        jnp.float32
    )
    replica_block_scales = jnp.einsum(
        "je,ebc->jbc", scale_select, all_scales, precision=lax.Precision.HIGHEST
    )
    return (quant_out, scale_out, hot_values, replica_block_scales)


def solution(mesh):
    n, reps = mesh.shape["ep"], mesh.shape["rep"]

    placed = (
        P("ep", "rep", None),
        P("ep", "rep", None),
        P("ep", None, "rep"),
        P("ep", "rep", None),
        P(),
        P(),
        P(),
    )
    outs = (
        P("ep", "rep", None),
        P("ep", "rep", None),
        P(None, ("rep", "ep"), None),
        P(None, "rep", None),
    )

    def run(quant_in, scale_in, b_train, a_train, adapter_ranks, trainer_map, hot_plan):
        shapes = [v.shape for v in (quant_in, scale_in, b_train, a_train)]
        local = functools.partial(kernel_body, n, reps) if fits(n, reps, *shapes) else body
        step = jax.shard_map(local, mesh=mesh, in_specs=placed, out_specs=outs, check_vma=False)
        return step(quant_in, scale_in, b_train, a_train, adapter_ranks, trainer_map, hot_plan)

    return run
```
